32 devices in a mesh: shard: 8 (over y, x, core), rep: 4 (over z).
Axes of the slice: x: 2, y: 2, z: 4, core: 2. Of those that a mesh axis runs over, the one named last changes fastest.
Arguments:
- latents: bfloat16 [32, 8, 2, 8, 1280], P(('shard', 'rep')), may hold values from -6 to 6
- depth_taps: bfloat16 [9, 1280], P(None, 'shard'), may hold values from -2 to 2
- time_taps: bfloat16 [3, 160, 1280], P(None, None, 'shard'), may hold values from -0.25 to 0.25
- cotangent: bfloat16 [32, 8, 2, 8, 1280], P(('shard', 'rep')), may hold values from -12 to 12, as said below
Outputs:
- block_out: bfloat16 [32, 8, 2, 8, 1280], P(('shard', 'rep'))
- input_grad: bfloat16 [32, 8, 2, 8, 1280], P(('shard', 'rep'))
- depth_grad: float32 [9, 1280], P(None, 'shard')
- time_grad: float32 [3, 160, 1280], P(None, None, 'shard')
The draws below stay inside these ranges and needn't reach their ends.
Inputs may be any that keep to these rules, and one draw needn't show every extreme that they name: Each clip's cotangent has a scale of its own.
All inputs are finite; a program needn't handle non-finite values.
Results may differ from the reference program's by a relative error of at most 0.003.
Values may be sent and summed in bfloat16 or wider, within the bound.
A program may use at most 64 MiB of HBM per device.

```python
import jax
import jax.numpy as jnp
from jax import lax

CH = 1280
GROUPS = 8
GW = 160
FR = 8
HT = 2
WD = 8
CLIPS = 32


def draw_cotangent(key, part):
    shape = (CLIPS, FR, HT, WD, CH)
    index = jnp.arange(CLIPS, dtype=jnp.float32)
    scale = jnp.power(3.0, index / max(CLIPS - 1, 1)).reshape(CLIPS, 1, 1, 1, 1)
    values = jax.random.truncated_normal(jax.random.fold_in(key, 13), -4.0, 4.0, shape, jnp.float32) * scale
    return values.astype(jnp.bfloat16)


def level_of(stream_key, extent, cuts, low, largest):
    def one(position, blocks):
        heights = jax.random.uniform(jax.random.fold_in(jax.random.fold_in(stream_key, 6), position), (blocks,), jnp.float32, low / len(cuts), largest / len(cuts))
        return jnp.repeat(jnp.exp(heights), extent[position] // blocks).reshape((-1,) + (1,) * (len(extent) - position - 1))

    gain = one(*cuts[0])
    for cut in cuts[1:]:
        gain = gain * one(*cut)
    return gain


def noise(own_key, shape, scale, reach, pieces=(), held_as=jnp.bfloat16):
    entries = jax.random.normal(own_key, shape, jnp.float32) * scale
    if len(pieces) > 0:
        entries = level_of(own_key, shape, pieces, -0.22, 0.18) * entries
    return jnp.clip(entries, min=-reach, max=reach).astype(held_as)


def setup_inputs(seed: int = 0) -> dict:
    streams_of = jax.random.split(jax.random.key(seed), 5)
    return {
        "latents": noise(streams_of[0], (CLIPS, FR, HT, WD, CH), 1.0, 6.0, ((0, 32),)),
        "depth_taps": noise(streams_of[1], (9, CH), 9 ** -0.5, 2.0, ((1, 8),)),
        "time_taps": noise(streams_of[2], (3, GW, CH), (3 * GW) ** -0.5, 0.25, ((2, 8),)),
        "cotangent": draw_cotangent(jax.random.fold_in(streams_of[4], 71), 0),
    }


def clip_pass(xc, dyc, depth_taps, time_taps):
    frames, rows, cols, chans = xc.shape
    width = chans // GROUPS
    wdf = depth_taps.astype(jnp.float32)
    xf = xc.astype(jnp.float32)
    xpad = jnp.pad(xf, ((0, 0), (1, 1), (1, 1), (0, 0)))
    spatial = jnp.zeros(xf.shape, jnp.float32)
    for i in range(3):
        for j in range(3):
            spatial = spatial + xpad[:, i:i + rows, j:j + cols] * wdf[3 * i + j]
    inv_rms = lax.rsqrt(lax.optimization_barrier(jnp.mean(spatial * spatial, -1, keepdims=True)) + 1e-05)
    normed = spatial * inv_rms
    activated = jax.nn.silu(normed).astype(jnp.bfloat16)
    act_grp = activated.astype(jnp.float32).reshape(frames, rows * cols, GROUPS, width)
    act_pad = jnp.pad(act_grp, ((1, 1), (0, 0), (0, 0), (0, 0)))
    taps = time_taps.astype(jnp.float32).reshape(3, width, GROUPS, width)
    temporal = jnp.zeros(act_grp.shape, jnp.float32)
    for k in range(3):
        temporal = temporal + jnp.einsum('fpgi,igo->fpgo', act_pad[k:k + frames], taps[k])
    block_out = (xf + temporal.reshape(xf.shape)).astype(jnp.bfloat16)
    dyf = dyc.astype(jnp.float32)
    dy_grp = dyf.reshape(frames, rows * cols, GROUPS, width)
    dy_pad = jnp.pad(dy_grp, ((1, 1), (0, 0), (0, 0), (0, 0)))
    act_grad = jnp.zeros(act_grp.shape, jnp.float32)
    time_terms = []
    for k in range(3):
        act_grad = act_grad + jnp.einsum('fpgo,igo->fpgi', dy_pad[2 - k:2 - k + frames], taps[k])
        time_terms.append(jnp.einsum('fpgi,fpgo->igo', act_pad[k:k + frames], dy_grp).reshape(width, chans))
    time_term = jnp.stack(time_terms)
    act_grad = act_grad.reshape(xf.shape)
    sig = jax.nn.sigmoid(normed)
    norm_grad = act_grad * sig * (1.0 + normed * (1.0 - sig))
    spatial_grad = inv_rms * (norm_grad - normed * lax.optimization_barrier(jnp.mean(norm_grad * normed, -1, keepdims=True)))
    grad_pad = jnp.pad(spatial_grad, ((0, 0), (1, 1), (1, 1), (0, 0)))
    input_grad = dyf
    depth_terms = []
    for i in range(3):
        for j in range(3):
            input_grad = input_grad + grad_pad[:, 2 - i:2 - i + rows, 2 - j:2 - j + cols] * wdf[3 * i + j]
            depth_terms.append(lax.optimization_barrier(jnp.sum(xpad[:, i:i + rows, j:j + cols] * spatial_grad, axis=(0, 1, 2))))
    depth_term = jnp.stack(depth_terms)
    return (block_out, input_grad.astype(jnp.bfloat16), depth_term, time_term)

def reference(latents, depth_taps, time_taps, cotangent):

    def step(carry, pair):
        out, grad_in, depth_term, time_term = clip_pass(pair[0], pair[1], depth_taps, time_taps)
        return ((carry[0] + depth_term, carry[1] + time_term), (out, grad_in))
    start = (jnp.zeros(depth_taps.shape, jnp.float32), jnp.zeros(time_taps.shape, jnp.float32))
    sums, outs = lax.scan(step, start, (latents, cotangent))
    scale = jnp.float32(1.0 / CLIPS)
    return (outs[0], outs[1], sums[0] * scale, sums[1] * scale)
```

```python
import functools

import jax
import jax.numpy as jnp
from jax import lax
from jax.experimental import pallas as pl
from jax.experimental.pallas import tpu as pltpu
from jax.sharding import PartitionSpec as P

GROUPS = 8


def moved(field, offset):
    if offset == 0:
        return field
    filler = jnp.zeros((field.shape[0], abs(offset)), field.dtype)
    if offset > 0:
        return jnp.concatenate([field[:, offset:], filler], 1)
    return jnp.concatenate([filler, field[:, :offset]], 1)


def inside(frames, height, breadth, frame_off, row_off, col_off):
    places = jnp.arange(frames * height * breadth, dtype=jnp.int32)
    frame_at = places // (height * breadth) + frame_off
    row_at = places // breadth % height + row_off
    col_at = places % breadth + col_off
    valid = (frame_at >= 0) & (frame_at < frames) & (row_at >= 0) & (row_at < height)
    valid = valid & (col_at >= 0) & (col_at < breadth)
    return valid[None, :]


def clip_pass(latent, cotan, depth_full, time_full):
    frames, height, breadth, chans = latent.shape
    plane = height * breadth
    count = frames * plane
    width = chans // GROUPS
    x_cols = latent.reshape(count, chans).T
    dy_cols = cotan.reshape(count, chans).T
    wdf = depth_full.astype(jnp.float32)
    spatial = jnp.zeros((chans, count), jnp.float32)
    for tap in range(9):
        row_off = tap // 3 - 1
        col_off = tap % 3 - 1
        offset = row_off * breadth + col_off
        shifted = jnp.where(
            inside(frames, height, breadth, 0, row_off, col_off), moved(x_cols, offset), 0
        )
        spatial = spatial + shifted * wdf[tap][:, None]
    inv_rms = lax.rsqrt(jnp.mean(spatial * spatial, 0, keepdims=True) + 1e-05)
    normed = spatial * inv_rms
    activated = jax.nn.silu(normed).astype(jnp.bfloat16)
    act_parts = []
    dy_parts = []
    for step in range(3):
        act_off = step - 1
        act_shift = jnp.where(
            inside(frames, height, breadth, act_off, 0, 0), moved(activated, act_off * plane), 0
        )
        act_parts.append(act_shift.reshape(GROUPS, width, count))
        dy_off = 1 - step
        dy_shift = jnp.where(
            inside(frames, height, breadth, dy_off, 0, 0), moved(dy_cols, dy_off * plane), 0
        )
        dy_parts.append(dy_shift.reshape(GROUPS, width, count))
    act_stack = jnp.concatenate(act_parts, 1)
    dy_stack = jnp.concatenate(dy_parts, 1)
    grouped = time_full.reshape(3, width, GROUPS, width)
    fwd_weight = grouped.transpose(2, 3, 0, 1).reshape(GROUPS, width, 3 * width)
    back_weight = grouped.transpose(2, 1, 0, 3).reshape(GROUPS, width, 3 * width)
    temporal = jnp.einsum(
        "goc,gcr->gor", fwd_weight, act_stack, preferred_element_type=jnp.float32
    ).reshape(chans, count)
    block_out = (x_cols.astype(jnp.float32) + temporal).astype(jnp.bfloat16)
    act_grad = jnp.einsum(
        "gic,gcr->gir", back_weight, dy_stack, preferred_element_type=jnp.float32
    ).reshape(chans, count)
    dy_group = dy_cols.reshape(GROUPS, width, count)
    time_term = jnp.einsum("gcr,gor->goc", act_stack, dy_group, preferred_element_type=jnp.float32)
    time_term = (
        time_term.reshape(GROUPS, width, 3, width).transpose(2, 3, 0, 1).reshape(3, width, chans)
    )
    sig = jax.nn.sigmoid(normed)
    norm_grad = act_grad * sig * (1.0 + normed * (1.0 - sig))
    spatial_grad = inv_rms * (norm_grad - normed * jnp.mean(norm_grad * normed, 0, keepdims=True))
    input_grad = dy_cols.astype(jnp.float32)
    depth_terms = []
    for tap in range(9):
        row_off = tap // 3 - 1
        col_off = tap % 3 - 1
        offset = row_off * breadth + col_off
        back_shift = jnp.where(
            inside(frames, height, breadth, 0, -row_off, -col_off),
            moved(spatial_grad, -offset),
            0.0,
        )
        input_grad = input_grad + back_shift * wdf[tap][:, None]
        shifted = jnp.where(
            inside(frames, height, breadth, 0, row_off, col_off), moved(x_cols, offset), 0
        )
        depth_terms.append(jnp.sum(shifted.astype(jnp.float32) * spatial_grad, axis=1))
    depth_term = jnp.stack(depth_terms)
    out_rows = block_out.T.reshape(latent.shape)
    grad_rows = input_grad.astype(jnp.bfloat16).T.reshape(latent.shape)
    return (out_rows, grad_rows, depth_term, time_term)


def per_device(latents, depth_taps, time_taps, cotangent):
    depth_full, time_full = (
        lax.all_gather(depth_taps, "shard", axis=1, tiled=True),
        lax.all_gather(time_taps, "shard", axis=2, tiled=True),
    )
    block_out, input_grad, depth_term, time_term = clip_pass(
        latents[0], cotangent[0], depth_full, time_full
    )
    scale = jnp.float32(1.0 / (lax.axis_size("shard") * lax.axis_size("rep")))
    depth_term = depth_term * scale
    time_term = time_term * scale
    time_part, depth_part = (
        lax.psum_scatter(time_term, "shard", scatter_dimension=2, tiled=True),
        lax.psum_scatter(depth_term, "shard", scatter_dimension=1, tiled=True),
    )
    time_grad, depth_grad = lax.psum((time_part, depth_part), "rep")
    return (block_out[None], input_grad[None], depth_grad, time_grad)


MESH = pl.DeviceIdType.MESH
LANES = 128


def window(group):
    return 128 * (group + group // 4)


def fused_kernel(
    n, reps, scale,
    x_hbm, dtaps_hbm, ttaps_hbm, dy_hbm,
    out_ref, gin_ref, dgrad_ref, tgrad_ref,
    x_ref, dtaps_ref, ttaps_ref, dy_ref, in_sem,
    sp, slope, ag, acc, act_pad, cot_pad, act_t, cot_t, act_all, cot_all, cot_sh,
    w_mine, w_in, w_all, d_mine, d_all, d_full,
    tg, tg_send, tg_recv, tg_out, dg, dg_send, dg_recv, dz_mine, dz_recv,
    d_ss, d_rs, c_ss, c_rs, a_ss, a_rs, w_ss, w_rs, f_ss, f_rs,
    r_ss, r_rs, g_ss, g_rs, p_ss, p_rs, q_ss, q_rs,
):
    frames, height, breadth, chans = sp.shape
    plane = height * breadth
    count = frames * plane
    width = chans // n
    tiles = chans // LANES
    me = lax.axis_index("shard")
    z = lax.axis_index("rep")
    sib = me + 1 - 2 * lax.rem(me, 2)
    shift = 32 * lax.rem(me, 4)

    def ahead(r):
        return lax.rem(me + r, n)

    def behind(r):
        return lax.rem(me + n - r, n)

    def zahead(r):
        return lax.rem(z + r, reps)

    def zbehind(r):
        return lax.rem(z + reps - r, reps)

    def remote(src, dst, ss, rs, **where):
        return pltpu.make_async_remote_copy(
            src_ref=src, dst_ref=dst, send_sem=ss, recv_sem=rs,
            device_id=where, device_id_type=MESH,
        )

    loads = [
        pltpu.make_async_copy(src, dst, in_sem.at[i])
        for i, (src, dst) in enumerate((
            (dtaps_hbm, dtaps_ref), (dy_hbm, dy_ref), (ttaps_hbm, ttaps_ref), (x_hbm, x_ref),
        ))
    ]
    for load in loads:
        load.start()
    barrier = pltpu.get_barrier_semaphore()
    for r in range(1, n):
        pl.semaphore_signal(barrier, inc=1, device_id={"shard": ahead(r)}, device_id_type=MESH)
    for r in range(1, reps):
        pl.semaphore_signal(barrier, inc=1, device_id={"rep": zahead(r)}, device_id_type=MESH)

    edge = jnp.zeros((plane, chans), jnp.bfloat16)
    act_pad[0:plane, :] = edge
    act_pad[count + plane:count + 2 * plane, :] = edge
    cot_pad[0:plane, :] = edge
    cot_pad[count + plane:count + 2 * plane, :] = edge
    for g in range(n):
        low = 32 * (g % 4)
        for k in range(3):
            if low > 0:
                w_all[g, k, 0:low, :] = jnp.zeros((low, 256), jnp.bfloat16)
            if low < 96:
                w_all[g, k, low + width:256, :] = jnp.zeros((96 - low, 256), jnp.bfloat16)
    ag[...] = jnp.zeros(ag.shape, jnp.float32)
    dg[...] = jnp.zeros(dg.shape, jnp.float32)
    cot_sh[3 * width:512, :] = jnp.zeros((512 - 3 * width, n * count), jnp.bfloat16)

    place = (
        lax.broadcasted_iota(jnp.int32, (width, 256), 1)
        == lax.broadcasted_iota(jnp.int32, (width, 256), 0) + shift
    ).astype(jnp.float32).astype(jnp.bfloat16)
    loads[0].wait()
    taps = jnp.concatenate(
        [dtaps_ref[...].astype(jnp.float32), jnp.zeros((7, width), jnp.float32)], axis=0
    ).astype(jnp.bfloat16)
    d_mine[...] = jnp.dot(taps, place, preferred_element_type=jnp.float32).astype(jnp.bfloat16)

    def cot_tile(t, carry):
        cols = pl.ds(pl.multiple_of(t * LANES, LANES), LANES)
        tile = dy_ref[0, :, :, :, cols].astype(jnp.float32).reshape(count, LANES)
        cot_pad[pl.ds(plane, count), cols] = tile.astype(jnp.bfloat16)
        cot_t[pl.ds(pl.multiple_of(t * LANES, LANES), LANES), :] = tile.T.astype(jnp.bfloat16)
        return carry

    loads[1].wait()
    lax.fori_loop(0, tiles, cot_tile, 0, unroll=2)
    loads[2].wait()
    row = lax.broadcasted_iota(jnp.int32, (width, LANES), 0)
    lane = lax.broadcasted_iota(jnp.int32, (width, LANES), 1)
    first = jnp.where((row < LANES) & (lax.rem(row + shift, LANES) == lane), 1.0, 0.0)
    first = first.astype(jnp.bfloat16)
    rest = jnp.zeros((width, LANES), jnp.float32)
    for k in range(3):
        spot = lax.rem(row + shift + 32 * k, LANES) == lane
        last = jnp.where((row >= LANES) & spot, 1.0, 0.0).astype(jnp.bfloat16)
        tap = ttaps_ref[k]
        w_mine[k] = jnp.dot(tap, first, preferred_element_type=jnp.float32).astype(jnp.bfloat16)
        rest = rest + jnp.dot(tap, last, preferred_element_type=jnp.float32)
    w_mine[3] = rest.astype(jnp.bfloat16)
    pl.semaphore_wait(barrier, n - 1 + reps - 1)

    d_copies = [
        remote(d_mine, d_all.at[me], d_ss.at[r - 1], d_rs.at[r - 1], shard=ahead(r))
        for r in range(1, n)
    ]
    for copy in d_copies:
        copy.start()

    def slab(p):
        return pl.ds(pl.multiple_of(p * width, 32), width)

    def lane_block(p):
        return pl.ds(pl.multiple_of(p * count, LANES), count)

    c_copies = [
        remote(
            cot_t.at[slab(ahead(r)), :], cot_all.at[:, lane_block(me)],
            c_ss.at[r - 1], c_rs.at[r - 1], shard=ahead(r),
        )
        for r in range(1, n)
    ]
    for copy in c_copies:
        copy.start()

    hops = list(range(2, n, 2))

    def w_send(c):
        cut = pl.ds(2 * c, 2)
        copies = [
            remote(w_mine.at[cut], w_in.at[me, cut], w_ss.at[c, i], w_rs.at[c, i], shard=ahead(r))
            for i, r in enumerate(hops)
        ]
        copies.append(remote(
            w_mine.at[cut], w_in.at[me, cut], w_ss.at[c, n // 2 - 1], w_rs.at[c, n // 2 - 1],
            shard=sib,
        ))
        for copy in copies:
            copy.start()
        return copies

    f_copies = []

    def w_pass(c):
        cut = pl.ds(2 * c, 2)
        for i, r in enumerate(hops):
            there = w_in.at[behind(r), cut]
            remote(w_mine.at[cut], there, w_ss.at[c, i], w_rs.at[c, i], shard=ahead(r)).wait_recv()
            f_copies.append(remote(there, there, f_ss.at[c, i], f_rs.at[c, i], shard=sib))
            f_copies[-1].start()

    w_copies = w_send(0)
    d_all[me] = d_mine[...]
    w_in[me] = w_mine[...]
    cot_all[:, lane_block(me)] = cot_t[slab(me), :]
    for r in range(1, n):
        remote(
            d_mine, d_all.at[behind(r)], d_ss.at[r - 1], d_rs.at[r - 1], shard=ahead(r)
        ).wait_recv()
    d_full[...] = jnp.zeros(d_full.shape, jnp.float32)
    for g in range(n):
        lo = window(g)
        d_full[:, lo:lo + 256] = d_full[:, lo:lo + 256] + d_all[g].astype(jnp.float32)

    column = lax.broadcasted_iota(jnp.int32, (frames, height, breadth, LANES), 2)

    def from_left(v):
        rolled = pltpu.roll(v.reshape(frames * height, breadth, LANES), 1, 1)
        return jnp.where(column == 0, 0.0, rolled.reshape(v.shape))

    def from_right(v):
        rolled = pltpu.roll(v.reshape(frames * height, breadth, LANES), breadth - 1, 1)
        return jnp.where(column == breadth - 1, 0.0, rolled.reshape(v.shape))

    def cols_of(t):
        return pl.ds(pl.multiple_of(t * LANES, LANES), LANES)

    def spatial_tile(t, carry):
        cols = cols_of(t)
        x = x_ref[0, :, :, :, cols].astype(jnp.float32)
        d = [d_full[k:k + 1, cols].reshape(1, 1, LANES) for k in range(9)]
        xs = [from_left(x), x, from_right(x)]
        top = sum(xs[j][:, 0] * d[3 + j] + xs[j][:, 1] * d[6 + j] for j in range(3))
        low = sum(xs[j][:, 0] * d[j] + xs[j][:, 1] * d[3 + j] for j in range(3))
        sp[:, 0, :, cols] = top
        sp[:, 1, :, cols] = low
        return (carry[0] + top * top, carry[1] + low * low)

    zero = jnp.zeros((frames, breadth, LANES), jnp.float32)
    loads[3].wait()
    squares = lax.fori_loop(0, tiles, spatial_tile, (zero, zero), unroll=2)
    inv = [
        lax.rsqrt(jnp.sum(s, axis=-1, keepdims=True) * (1.0 / chans) + 1e-05) for s in squares
    ]
    inv_rms = jnp.concatenate([v[:, None] for v in inv], axis=1)

    def act_tile(t, carry):
        cols = cols_of(t)
        normed = sp[:, :, :, cols] * inv_rms
        sig = jax.nn.sigmoid(normed)
        sp[:, :, :, cols] = normed
        slope[:, :, :, cols] = sig * (1.0 + normed * (1.0 - sig))
        tile = (normed * sig).reshape(count, LANES)
        act_pad[pl.ds(plane, count), cols] = tile.astype(jnp.bfloat16)
        act_t[cols, :] = tile.T.astype(jnp.bfloat16)
        return carry

    lax.fori_loop(0, tiles, act_tile, 0, unroll=2)

    a_copies = [
        remote(
            act_t.at[slab(ahead(r)), :], act_all.at[:, lane_block(me)],
            a_ss.at[r - 1], a_rs.at[r - 1], shard=ahead(r),
        )
        for r in range(1, n)
    ]
    for copy in a_copies:
        copy.start()
    w_copies += w_send(1)
    act_all[:, lane_block(me)] = act_t[slab(me), :]

    for r in range(1, n):
        remote(
            cot_t.at[slab(me), :], cot_all.at[:, lane_block(behind(r))],
            c_ss.at[r - 1], c_rs.at[r - 1], shard=ahead(r),
        ).wait_recv()
    src = lax.broadcasted_iota(jnp.int32, (count, 2 * count), 0)
    dst = lax.broadcasted_iota(jnp.int32, (count, 2 * count), 1)
    target = dst + jnp.where(dst < count, plane, -plane - count)
    mover = jnp.where(src == target, 1.0, 0.0).astype(jnp.bfloat16)
    for c in range(n):
        lanes = slice(c * count, (c + 1) * count)
        moved_cot = jnp.dot(cot_all[:, lanes], mover, preferred_element_type=jnp.float32)
        cot_sh[0:width, lanes] = moved_cot[:, :count].astype(jnp.bfloat16)
        cot_sh[width:2 * width, lanes] = cot_all[:, lanes]
        cot_sh[2 * width:3 * width, lanes] = moved_cot[:, count:].astype(jnp.bfloat16)
    for r in range(1, n):
        remote(
            act_t.at[slab(me), :], act_all.at[:, lane_block(behind(r))],
            a_ss.at[r - 1], a_rs.at[r - 1], shard=ahead(r),
        ).wait_recv()
    nt = (((1,), (1,)), ((), ()))
    part = width // reps
    product = lax.dot_general(act_all[...], cot_sh[...], nt, preferred_element_type=jnp.float32)
    tg[...] = product.reshape(reps, part, 512)
    tg_send[...] = tg[...].astype(jnp.bfloat16)
    r_copies = [
        remote(
            tg_send.at[zahead(r)], tg_recv.at[r - 1], r_ss.at[r - 1], r_rs.at[r - 1],
            rep=zahead(r),
        )
        for r in range(1, reps)
    ]
    for copy in r_copies:
        copy.start()

    nn = (((1,), (0,)), ((), ()))
    lane = lax.broadcasted_iota(jnp.int32, (width, LANES), 1)

    def mask(hit):
        return jnp.where(hit, 1.0, 0.0).astype(jnp.bfloat16)

    def group_grad(p):
        off = 32 * lax.rem(p, 4)
        rows = pl.ds(pl.multiple_of(off, 32), width)
        near, far = mask(lane >= off), mask(lane < off)
        tail = mask((lane >= off) & (lane < off + 32))
        rest = w_in[p, 3].astype(jnp.float32)
        for k in range(3):
            turned = rest if k == 0 else pltpu.roll(rest, LANES - 32 * k, 1)
            main = w_in[p, k]
            w_all[p, k, rows, 0:LANES] = main * near
            w_all[p, k, rows, LANES:256] = main * far + turned.astype(jnp.bfloat16) * tail
        lanes = pl.ds(pl.multiple_of(window(p), LANES), 256)
        term = sum(
            lax.dot_general(
                cot_pad[plane * (2 - k):plane * (2 - k) + count, lanes], w_all[p, k], nt,
                preferred_element_type=jnp.float32,
            )
            for k in range(3)
        )
        ag[:, lanes] = ag[:, lanes] + term

    w_pass(0)
    group_grad(me)
    w_pass(1)

    for c in range(2):
        cut = pl.ds(2 * c, 2)
        remote(w_mine.at[cut], w_in.at[sib, cut], w_ss.at[c, n // 2 - 1], w_rs.at[c, n // 2 - 1],
               shard=sib).wait_recv()
    group_grad(sib)
    for r in hops:
        group_grad(behind(r))
    for i, r in enumerate(hops):
        p = lax.rem(sib + n - r, n)
        for c in range(2):
            there = w_in.at[p, pl.ds(2 * c, 2)]
            remote(there, there, f_ss.at[c, i], f_rs.at[c, i], shard=sib).wait_recv()
        group_grad(p)

    def grouped(source, order, weight_dims, store):
        for g in range(n):
            lo = window(g)
            term = sum(
                lax.dot_general(
                    source[plane * order(k):plane * order(k) + count, lo:lo + 256],
                    w_all[g, k], weight_dims, preferred_element_type=jnp.float32,
                )
                for k in range(3)
            )
            if g % 4 == 0:
                store[:, lo:lo + 256] = term
            else:
                store[:, lo:lo + 128] = store[:, lo:lo + 128] + term[:, :128]
                store[:, lo + 128:lo + 256] = term[:, 128:]

    def norm_tile(t, carry):
        cols = cols_of(t)
        grad = ag[:, cols].reshape(frames, height, breadth, LANES) * slope[:, :, :, cols]
        ag[:, cols] = grad.reshape(count, LANES)
        return carry + grad * sp[:, :, :, cols]

    dots = lax.fori_loop(
        0, tiles, norm_tile, jnp.zeros((frames, height, breadth, LANES), jnp.float32), unroll=2)
    mean = jnp.sum(dots, axis=-1, keepdims=True) * (1.0 / chans)


    def depth_tile(t, carry):
        cols = cols_of(t)
        grad = ag[:, cols].reshape(frames, height, breadth, LANES)
        sg = inv_rms * (grad - sp[:, :, :, cols] * mean)
        ag[:, cols] = sg.reshape(count, LANES)
        gs = [from_right(sg), sg, from_left(sg)]
        x = x_ref[0, :, :, :, cols].astype(jnp.float32)
        x0, x1 = x[:, 0], x[:, 1]
        for j in range(3):
            g0, g1 = gs[j][:, 0], gs[j][:, 1]
            for i, term in enumerate((x0 * g1, x0 * g0 + x1 * g1, x1 * g0)):
                dg[3 * i + j:3 * i + j + 1, cols] = jnp.sum(
                    jnp.sum(term, axis=0), axis=0, keepdims=True
                )
        return carry

    lax.fori_loop(0, tiles, depth_tile, 0, unroll=2)

    def grad_tile(t, carry):
        cols = cols_of(t)
        sg = ag[:, cols].reshape(frames, height, breadth, LANES)
        d = [d_full[k:k + 1, cols].reshape(1, 1, LANES) for k in range(9)]
        gs = [from_right(sg), sg, from_left(sg)]
        top = dy_ref[0, :, 0, :, cols].astype(jnp.float32)
        low = dy_ref[0, :, 1, :, cols].astype(jnp.float32)
        for j in range(3):
            g0, g1 = gs[j][:, 0], gs[j][:, 1]
            top = top + g0 * d[3 + j] + g1 * d[j]
            low = low + g0 * d[6 + j] + g1 * d[3 + j]
        gin_ref[0, :, 0, :, cols] = top.astype(jnp.bfloat16)
        gin_ref[0, :, 1, :, cols] = low.astype(jnp.bfloat16)
        return carry

    def dwin(p):
        return pl.ds(pl.multiple_of(window(p), LANES), 256)

    dg_send[...] = dg[...].astype(jnp.bfloat16)
    p_copies = [
        remote(dg_send.at[:, dwin(ahead(r))], dg_recv.at[me], p_ss.at[r - 1], p_rs.at[r - 1],
               shard=ahead(r))
        for r in range(1, n)
    ]
    for copy in p_copies:
        copy.start()
    dg_recv[me] = dg_send[:, dwin(me)]

    for r in range(1, reps):
        r_copies[r - 1].wait_recv()
    total = tg[z]
    for r in range(1, reps):
        total = total + tg_recv[r - 1].astype(jnp.float32)
    tg_out[z] = (total * scale).astype(jnp.bfloat16)
    g_copies = [
        remote(tg_out.at[z], tg_out.at[z], g_ss.at[r - 1], g_rs.at[r - 1], rep=zahead(r))
        for r in range(1, reps)
    ]
    for copy in g_copies:
        copy.start()

    grouped(act_pad, lambda k: k, nn, acc)

    def depth_first():
        for r in range(1, n):
            remote(dg_send.at[:, dwin(me)], dg_recv.at[behind(r)], p_ss.at[r - 1], p_rs.at[r - 1],
                   shard=ahead(r)).wait_recv()
        total = dg_recv[0].astype(jnp.float32)
        for p in range(1, n):
            total = total + dg_recv[p].astype(jnp.float32)
        dz_mine[...] = total.astype(jnp.bfloat16)
        copies = [
            remote(dz_mine, dz_recv.at[z], q_ss.at[r - 1], q_rs.at[r - 1], rep=zahead(r))
            for r in range(1, reps)
        ]
        for copy in copies:
            copy.start()
        dz_recv[z] = dz_mine[...]
        return copies

    q_copies = depth_first()
    lax.fori_loop(0, tiles, grad_tile, 0, unroll=2)

    def out_tile(t, carry):
        cols = cols_of(t)
        x = x_ref[0, :, :, :, cols].astype(jnp.float32)
        y = x + acc[:, cols].reshape(frames, height, breadth, LANES)
        out_ref[0, :, :, :, cols] = y.astype(jnp.bfloat16)
        return carry

    lax.fori_loop(0, tiles, out_tile, 0, unroll=2)

    for r in range(1, reps):
        remote(tg_out.at[z], tg_out.at[zbehind(r)], g_ss.at[r - 1], g_rs.at[r - 1],
               rep=zahead(r)).wait_recv()
    grads = tg_out[...].astype(jnp.float32).reshape(width, 512)
    for k in range(3):
        tgrad_ref[k] = grads[:, k * width:(k + 1) * width]

    for r in range(1, reps):
        remote(dz_mine, dz_recv.at[zbehind(r)], q_ss.at[r - 1], q_rs.at[r - 1],
               rep=zahead(r)).wait_recv()
    whole = dz_recv[0].astype(jnp.float32)
    for r in range(1, reps):
        whole = whole + dz_recv[r].astype(jnp.float32)
    whole = pltpu.roll(whole * scale, lax.rem(256 - shift, 256), 1)
    dgrad_ref[...] = whole[0:9, 0:width]

    for copies in (d_copies, c_copies, a_copies, w_copies, f_copies, r_copies, g_copies,
                   p_copies, q_copies):
        for copy in copies:
            copy.wait_send()


def fused_device(latents, depth_taps, time_taps, cotangent):
    n, reps = lax.axis_size("shard"), lax.axis_size("rep")
    _, frames, height, breadth, chans = latents.shape
    count = frames * height * breadth
    padded = count + 2 * height * breadth
    width = chans // n
    bf, f32 = jnp.bfloat16, jnp.float32
    dma = pltpu.SemaphoreType.DMA
    part = width // reps
    vmem = pl.BlockSpec(memory_space=pltpu.VMEM)
    results = pl.pallas_call(
        functools.partial(fused_kernel, n, reps, 1.0 / (n * reps)),
        out_shape=(
            pltpu.VMEM(latents.shape, bf),
            pltpu.VMEM(latents.shape, bf),
            pltpu.VMEM((9, width), f32),
            pltpu.VMEM((3, width, width), f32),
        ),
        in_specs=[pl.BlockSpec(memory_space=pltpu.HBM)] * 4,
        out_specs=[vmem] * 4,
        scratch_shapes=[
            pltpu.VMEM(latents.shape, bf),
            pltpu.VMEM(depth_taps.shape, bf),
            pltpu.VMEM(time_taps.shape, bf),
            pltpu.VMEM(cotangent.shape, bf),
            dma((4,)),
            pltpu.VMEM((frames, height, breadth, chans), f32),
            pltpu.VMEM((frames, height, breadth, chans), f32),
            pltpu.VMEM((count, chans), f32),
            pltpu.VMEM((count, chans), f32),
            pltpu.VMEM((padded, chans), bf),
            pltpu.VMEM((padded, chans), bf),
            pltpu.VMEM((chans, count), bf),
            pltpu.VMEM((chans, count), bf),
            pltpu.VMEM((width, n * count), bf),
            pltpu.VMEM((width, n * count), bf),
            pltpu.VMEM((512, n * count), bf),
            pltpu.VMEM((4, width, LANES), bf),
            pltpu.VMEM((n, 4, width, LANES), bf),
            pltpu.VMEM((n, 3, 256, 256), bf),
            pltpu.VMEM((16, 256), bf),
            pltpu.VMEM((n, 16, 256), bf),
            pltpu.VMEM((16, chans), f32),
            pltpu.VMEM((reps, part, 512), f32),
            pltpu.VMEM((reps, part, 512), bf),
            pltpu.VMEM((reps - 1, part, 512), bf),
            pltpu.VMEM((reps, part, 512), bf),
            pltpu.VMEM((16, chans), f32),
            pltpu.VMEM((16, chans), bf),
            pltpu.VMEM((n, 16, 256), bf),
            pltpu.VMEM((16, 256), bf),
            pltpu.VMEM((reps, 16, 256), bf),
            dma((n - 1,)), dma((n - 1,)),
            dma((n - 1,)), dma((n - 1,)),
            dma((n - 1,)), dma((n - 1,)),
            dma((2, n // 2)), dma((2, n // 2)),
            dma((2, n // 2 - 1)), dma((2, n // 2 - 1)),
            dma((reps - 1,)), dma((reps - 1,)),
            dma((reps - 1,)), dma((reps - 1,)),
            dma((n - 1,)), dma((n - 1,)),
            dma((reps - 1,)), dma((reps - 1,)),
        ],
        compiler_params=pltpu.CompilerParams(
            collective_id=0, has_side_effects=True, vmem_limit_bytes=24 * 1024 * 1024
        ),
    )(*[pltpu.with_memory_space_constraint(a, pltpu.HBM)
        for a in (latents, depth_taps, time_taps, cotangent)])
    return store_out(results)


def store_kernel(*refs):
    sources, targets, sems = refs[:4], refs[4:8], refs[8]
    copies = [
        pltpu.make_async_copy(source, target, sems.at[i])
        for i, (source, target) in enumerate(zip(sources, targets))
    ]
    for copy in copies:
        copy.start()
    for copy in copies:
        copy.wait()


def store_out(results):
    return pl.pallas_call(
        store_kernel,
        out_shape=tuple(jax.ShapeDtypeStruct(r.shape, r.dtype) for r in results),
        in_specs=[pl.BlockSpec(memory_space=pltpu.VMEM)] * 4,
        out_specs=[pl.BlockSpec(memory_space=pltpu.HBM)] * 4,
        scratch_shapes=[pltpu.SemaphoreType.DMA((4,))],
        compiler_params=pltpu.CompilerParams(has_side_effects=True),
    )(*[pltpu.with_memory_space_constraint(r, pltpu.VMEM) for r in results])


def solution(mesh):
    placed = (
        P(("shard", "rep"), None, None, None, None),
        P(None, "shard"),
        P(None, None, "shard"),
        P(("shard", "rep"), None, None, None, None),
    )
    shards, reps = mesh.shape["shard"], mesh.shape["rep"]
    fused = shards == GROUPS and reps in (2, 4)
    return jax.shard_map(
        fused_device if fused else per_device,
        mesh=mesh,
        in_specs=placed,
        out_specs=(
            P(("shard", "rep"), None, None, None, None),
            P(("shard", "rep"), None, None, None, None),
            P(None, "shard"),
            P(None, None, "shard"),
        ),
        check_vma=False,
    )
```

```python
import functools

import jax
import jax.numpy as jnp
from jax import lax
from jax.experimental import pallas as pl
from jax.experimental.pallas import tpu as pltpu
from jax.sharding import PartitionSpec as P

GROUPS = 8


def moved(field, offset):
    if offset == 0:
        return field
    filler = jnp.zeros((field.shape[0], abs(offset)), field.dtype)
    if offset > 0:
        return jnp.concatenate([field[:, offset:], filler], 1)
    return jnp.concatenate([filler, field[:, :offset]], 1)


def inside(frames, height, breadth, frame_off, row_off, col_off):
    places = jnp.arange(frames * height * breadth, dtype=jnp.int32)
    frame_at = places // (height * breadth) + frame_off
    row_at = places // breadth % height + row_off
    col_at = places % breadth + col_off
    valid = (frame_at >= 0) & (frame_at < frames) & (row_at >= 0) & (row_at < height)
    valid = valid & (col_at >= 0) & (col_at < breadth)
    return valid[None, :]


def clip_pass(latent, cotan, depth_full, time_full):
    frames, height, breadth, chans = latent.shape
    plane = height * breadth
    count = frames * plane
    width = chans // GROUPS
    x_cols = latent.reshape(count, chans).T
    dy_cols = cotan.reshape(count, chans).T
    wdf = depth_full.astype(jnp.float32)
    spatial = jnp.zeros((chans, count), jnp.float32)
    for tap in range(9):
        row_off = tap // 3 - 1
        col_off = tap % 3 - 1
        offset = row_off * breadth + col_off
        shifted = jnp.where(
            inside(frames, height, breadth, 0, row_off, col_off), moved(x_cols, offset), 0
        )
        spatial = spatial + shifted * wdf[tap][:, None]
    inv_rms = lax.rsqrt(jnp.mean(spatial * spatial, 0, keepdims=True) + 1e-05)
    normed = spatial * inv_rms
    activated = jax.nn.silu(normed).astype(jnp.bfloat16)
    act_parts = []
    dy_parts = []
    for step in range(3):
        act_off = step - 1
        act_shift = jnp.where(
            inside(frames, height, breadth, act_off, 0, 0), moved(activated, act_off * plane), 0
        )
        act_parts.append(act_shift.reshape(GROUPS, width, count))
        dy_off = 1 - step
        dy_shift = jnp.where(
            inside(frames, height, breadth, dy_off, 0, 0), moved(dy_cols, dy_off * plane), 0
        )
        dy_parts.append(dy_shift.reshape(GROUPS, width, count))
    act_stack = jnp.concatenate(act_parts, 1)
    dy_stack = jnp.concatenate(dy_parts, 1)
    grouped = time_full.reshape(3, width, GROUPS, width)
    fwd_weight = grouped.transpose(2, 3, 0, 1).reshape(GROUPS, width, 3 * width)
    back_weight = grouped.transpose(2, 1, 0, 3).reshape(GROUPS, width, 3 * width)
    temporal = jnp.einsum(
        "goc,gcr->gor", fwd_weight, act_stack, preferred_element_type=jnp.float32
    ).reshape(chans, count)
    block_out = (x_cols.astype(jnp.float32) + temporal).astype(jnp.bfloat16)
    act_grad = jnp.einsum(
        "gic,gcr->gir", back_weight, dy_stack, preferred_element_type=jnp.float32
    ).reshape(chans, count)
    dy_group = dy_cols.reshape(GROUPS, width, count)
    time_term = jnp.einsum("gcr,gor->goc", act_stack, dy_group, preferred_element_type=jnp.float32)
    time_term = (
        time_term.reshape(GROUPS, width, 3, width).transpose(2, 3, 0, 1).reshape(3, width, chans)
    )
    sig = jax.nn.sigmoid(normed)
    norm_grad = act_grad * sig * (1.0 + normed * (1.0 - sig))
    spatial_grad = inv_rms * (norm_grad - normed * jnp.mean(norm_grad * normed, 0, keepdims=True))
    input_grad = dy_cols.astype(jnp.float32)
    depth_terms = []
    for tap in range(9):
        row_off = tap // 3 - 1
        col_off = tap % 3 - 1
        offset = row_off * breadth + col_off
        back_shift = jnp.where(
            inside(frames, height, breadth, 0, -row_off, -col_off),
            moved(spatial_grad, -offset),
            0.0,
        )
        input_grad = input_grad + back_shift * wdf[tap][:, None]
        shifted = jnp.where(
            inside(frames, height, breadth, 0, row_off, col_off), moved(x_cols, offset), 0
        )
        depth_terms.append(jnp.sum(shifted.astype(jnp.float32) * spatial_grad, axis=1))
    depth_term = jnp.stack(depth_terms)
    out_rows = block_out.T.reshape(latent.shape)
    grad_rows = input_grad.astype(jnp.bfloat16).T.reshape(latent.shape)
    return (out_rows, grad_rows, depth_term, time_term)


def per_device(latents, depth_taps, time_taps, cotangent):
    depth_full, time_full = (
        lax.all_gather(depth_taps, "shard", axis=1, tiled=True),
        lax.all_gather(time_taps, "shard", axis=2, tiled=True),
    )
    block_out, input_grad, depth_term, time_term = clip_pass(
        latents[0], cotangent[0], depth_full, time_full
    )
    scale = jnp.float32(1.0 / (lax.axis_size("shard") * lax.axis_size("rep")))
    depth_term = depth_term * scale
    time_term = time_term * scale
    time_part, depth_part = (
        lax.psum_scatter(time_term, "shard", scatter_dimension=2, tiled=True),
        lax.psum_scatter(depth_term, "shard", scatter_dimension=1, tiled=True),
    )
    time_grad, depth_grad = lax.psum((time_part, depth_part), "rep")
    return (block_out[None], input_grad[None], depth_grad, time_grad)


MESH = pl.DeviceIdType.MESH
LANES = 128
PEERS = (1, 6, 2, 4, 7, 3, 5)
CHUNKS = 2


def window(group):
    return 128 * (group + group // 4)


def fused_kernel(
    n, reps, scale,
    x_hbm, dtaps_hbm, ttaps_hbm, dy_hbm,
    out_ref, gin_ref, dgrad_ref, tgrad_ref,
    x_ref, dtaps_ref, ttaps_ref, dy_ref, in_sem,
    sp, slope, ag, act_t, cot_t, act_all, cot_all, cot_sh,
    w_fwd, ret_send, ret_all, tem_send, tem_all,
    d_mine, d_all, d_full,
    tg, tg_send, tg_recv, tg_out, dg, dg_send, dg_recv, dz_mine, dz_recv,
    sent, d_rs, c_rs, a_rs, b_rs, t_rs, r_rs, g_rs, p_rs, q_rs,
):
    frames, height, breadth, chans = sp.shape
    plane = height * breadth
    count = frames * plane
    width = chans // n
    tiles = chans // LANES
    piece = width // CHUNKS
    me = lax.axis_index("shard")
    z = lax.axis_index("rep")
    shift = 32 * lax.rem(me, 4)
    turns = [1 - 2 * lax.rem(lax.div(me, 1 << b), 2) for b in range(3)]
    peers = {m: me + sum((1 << b) * turns[b] for b in range(3) if m >> b & 1) for m in PEERS}

    def zahead(r):
        return lax.rem(z + r, reps)

    def remote(src, dst, ss, rs, **where):
        return pltpu.make_async_remote_copy(
            src_ref=src, dst_ref=dst, send_sem=ss, recv_sem=rs,
            device_id=where, device_id_type=MESH,
        )

    def start(copies):
        for copy in copies:
            copy.start()

    def arrive(ref, sem):
        pltpu.make_async_copy(ref, ref, sem).wait()

    loads = [
        pltpu.make_async_copy(src, dst, in_sem.at[i])
        for i, (src, dst) in enumerate((
            (dtaps_hbm, dtaps_ref), (dy_hbm, dy_ref), (ttaps_hbm, ttaps_ref), (x_hbm, x_ref),
        ))
    ]
    for load in loads:
        load.start()
    barrier = pltpu.get_barrier_semaphore()
    for r in range(1, reps):
        pl.semaphore_signal(barrier, inc=1, device_id={"rep": zahead(r)}, device_id_type=MESH)
    for m in PEERS:
        pl.semaphore_signal(barrier, inc=1, device_id={"shard": peers[m]}, device_id_type=MESH)

    dg[...] = jnp.zeros(dg.shape, jnp.float32)
    cot_sh[3 * width:512, :] = jnp.zeros((512 - 3 * width, n * count), jnp.bfloat16)

    place = (
        lax.broadcasted_iota(jnp.int32, (width, 256), 1)
        == lax.broadcasted_iota(jnp.int32, (width, 256), 0) + shift
    ).astype(jnp.float32).astype(jnp.bfloat16)
    loads[0].wait()
    taps = jnp.concatenate(
        [dtaps_ref[...].astype(jnp.float32), jnp.zeros((7, width), jnp.float32)], axis=0
    ).astype(jnp.bfloat16)
    d_mine[...] = jnp.dot(taps, place, preferred_element_type=jnp.float32).astype(jnp.bfloat16)

    def cols_of(t):
        return pl.ds(pl.multiple_of(t * LANES, LANES), LANES)

    def cot_tile(t, carry):
        cols = cols_of(t)
        tile = dy_ref[0, :, :, :, cols].astype(jnp.float32).reshape(count, LANES)
        cot_t[cols, :] = tile.T.astype(jnp.bfloat16)
        return carry

    loads[1].wait()
    lax.fori_loop(0, tiles, cot_tile, 0, unroll=2)
    nt = (((1,), (1,)), ((), ()))
    loads[2].wait()
    same = (
        lax.broadcasted_iota(jnp.int32, (width, width), 0)
        == lax.broadcasted_iota(jnp.int32, (width, width), 1)
    ).astype(jnp.float32).astype(jnp.bfloat16)
    for k in range(3):
        w_fwd[k] = lax.dot_general(
            same, ttaps_ref[k], nt, preferred_element_type=jnp.float32
        ).astype(jnp.bfloat16)
    pl.semaphore_wait(barrier, n - 1 + reps - 1)

    def slab(p):
        return pl.ds(pl.multiple_of(p * width, 32), width)

    def d_copy(m, origin):
        return remote(d_mine, d_all.at[origin], sent.at[0], d_rs, shard=peers[m])

    def c_copy(m, origin):
        return remote(
            cot_t.at[slab(peers[m]), :], cot_all.at[origin],
            sent.at[1], c_rs.at[m // 2], shard=peers[m],
        )

    def a_copy(h, m, origin):
        rows = pl.ds(pl.multiple_of(peers[m] * width + piece * h, 16), piece)
        return remote(
            act_t.at[rows, :], act_all.at[origin, pl.ds(piece * h, piece)],
            sent.at[2], a_rs.at[h], shard=peers[m],
        )

    def b_copy(m, origin):
        return remote(
            ret_send.at[peers[m]], ret_all.at[slab(origin), :],
            sent.at[3], b_rs, shard=peers[m],
        )

    def t_copy(m, origin):
        return remote(
            tem_send.at[peers[m]], tem_all.at[slab(origin), :],
            sent.at[4], t_rs, shard=peers[m],
        )

    start([d_copy(m, me) for m in PEERS])
    start([c_copy(m, me) for m in PEERS])
    d_all[me] = d_mine[...]
    cot_all[me] = cot_t[slab(me), :]

    lane = lax.broadcasted_iota(jnp.int32, (width, count), 1)

    def later(v):
        return jnp.where(lane < count - plane, pltpu.roll(v, count - plane, 1), 0.0)

    def earlier(v):
        return jnp.where(lane >= plane, pltpu.roll(v, plane, 1), 0.0)

    def clipwise(step, v):
        clips = v.shape[1] // count
        return jnp.concatenate([step(v[:, i * count:(i + 1) * count]) for i in range(clips)], axis=1)

    def chip(p):
        return lax.div(p, 2) * 2

    def temporal(source, weights, first, clips, step, other, target):
        block = jnp.concatenate([source[first + i] for i in range(clips)], axis=1)
        terms = jnp.dot(
            weights[...].reshape(3 * width, width), block, preferred_element_type=jnp.float32
        )
        start_term, end_term = clipwise(step, terms[0:width]), clipwise(other, terms[2 * width:])
        total = (start_term + terms[width:2 * width] + end_term).astype(jnp.bfloat16)
        for i in range(clips):
            target[first + i] = total[:, i * count:(i + 1) * count]
        return block

    def back(first, clips):
        block = temporal(cot_all, ttaps_ref, first, clips, later, earlier, ret_send)
        lanes = pl.ds(pl.multiple_of(first * count, count * clips), count * clips)
        wide = block.astype(jnp.float32)
        cot_sh[0:width, lanes] = clipwise(later, wide).astype(jnp.bfloat16)
        cot_sh[width:2 * width, lanes] = block
        cot_sh[2 * width:3 * width, lanes] = clipwise(earlier, wide).astype(jnp.bfloat16)

    def forth(first):
        temporal(act_all, w_fwd, first, 2, earlier, later, tem_send)

    def give_back(*masks):
        clips = len(masks)
        first = peers[masks[0]] if clips == 1 else chip(peers[masks[0]])
        arrive(cot_all.at[pl.ds(first, clips)], c_rs.at[masks[0] // 2])
        back(first, clips)
        start([b_copy(m, me) for m in masks])

    back(me, 1)
    ret_all[slab(me), :] = ret_send[me]
    give_back(1)

    arrive(d_all.at[0:n - 1], d_rs)
    d_full[...] = jnp.zeros(d_full.shape, jnp.float32)
    for g in range(n):
        lo = window(g)
        d_full[:, lo:lo + 256] = d_full[:, lo:lo + 256] + d_all[g].astype(jnp.float32)

    column = lax.broadcasted_iota(jnp.int32, (frames, height, breadth, LANES), 2)

    def from_left(v):
        rolled = pltpu.roll(v.reshape(frames * height, breadth, LANES), 1, 1)
        return jnp.where(column == 0, 0.0, rolled.reshape(v.shape))

    def from_right(v):
        rolled = pltpu.roll(v.reshape(frames * height, breadth, LANES), breadth - 1, 1)
        return jnp.where(column == breadth - 1, 0.0, rolled.reshape(v.shape))

    def spatial_tile(t, carry):
        cols = cols_of(t)
        x = x_ref[0, :, :, :, cols].astype(jnp.float32)
        d = [d_full[k:k + 1, cols].reshape(1, 1, LANES) for k in range(9)]
        xs = [from_left(x), x, from_right(x)]
        top = sum(xs[j][:, 0] * d[3 + j] + xs[j][:, 1] * d[6 + j] for j in range(3))
        low = sum(xs[j][:, 0] * d[j] + xs[j][:, 1] * d[3 + j] for j in range(3))
        sp[:, 0, :, cols] = top
        sp[:, 1, :, cols] = low
        return (carry[0] + top * top, carry[1] + low * low)

    zero = jnp.zeros((frames, breadth, LANES), jnp.float32)
    loads[3].wait()
    squares = lax.fori_loop(0, tiles, spatial_tile, (zero, zero), unroll=2)
    inv = [
        lax.rsqrt(jnp.sum(s, axis=-1, keepdims=True) * (1.0 / chans) + 1e-05) for s in squares
    ]
    inv_rms = jnp.concatenate([v[:, None] for v in inv], axis=1)

    def act_tile(t, carry):
        cols = cols_of(t)
        normed = sp[:, :, :, cols] * inv_rms
        sig = jax.nn.sigmoid(normed)
        sp[:, :, :, cols] = normed
        slope[:, :, :, cols] = sig * (1.0 + normed * (1.0 - sig))
        tile = (normed * sig).reshape(count, LANES)
        act_t[cols, :] = tile.T.astype(jnp.bfloat16)
        return carry

    lax.fori_loop(0, tiles, act_tile, 0, unroll=2)
    for h in range(CHUNKS):
        start([a_copy(h, m, me) for m in PEERS])
    act_all[me] = act_t[slab(me), :]
    give_back(2, 3)
    give_back(4, 5)
    give_back(6, 7)

    def time_product(h):
        rows = slice(piece * h, piece * (h + 1))
        arrive(act_all.at[0:n - 1, rows], a_rs.at[h])
        acts = jnp.concatenate([act_all[p, rows] for p in range(n)], axis=1)
        product = lax.dot_general(acts, cot_sh[...], nt, preferred_element_type=jnp.float32)
        for q in range(reps):
            block = product[:, q * 512 // reps:(q + 1) * 512 // reps]
            tg[h, q] = block
            tg_send[h, q] = block.astype(jnp.bfloat16)
        start([
            remote(
                tg_send.at[h, zahead(r)], tg_recv.at[h, r - 1], sent.at[5], r_rs.at[h],
                rep=zahead(r),
            )
            for r in range(1, reps)
        ])

    def time_sum(h):
        arrive(tg_recv.at[h], r_rs.at[h])
        total = tg[h, z]
        for r in range(1, reps):
            total = total + tg_recv[h, r - 1].astype(jnp.float32)
        tg_out[h, z] = (total * scale).astype(jnp.bfloat16)
        start([
            remote(
                tg_out.at[h, z], tg_out.at[h, z], sent.at[6], g_rs.at[h], rep=zahead(r),
            )
            for r in range(1, reps)
        ])

    for h in range(CHUNKS):
        time_product(h)
    for m in (6, 2, 4):
        forth(chip(peers[m]))
        start([t_copy(m, me), t_copy(m + 1, me)])
    forth(chip(me))
    start([t_copy(1, me)])
    tem_all[slab(me), :] = tem_send[me]
    arrive(ret_all.at[0:(n - 1) * width, :], b_rs)

    def norm_tile(t, carry):
        cols = cols_of(t)
        back_rows = ret_all[cols, :].astype(jnp.float32).T
        grad = back_rows.reshape(frames, height, breadth, LANES) * slope[:, :, :, cols]
        ag[:, cols] = grad.reshape(count, LANES)
        return carry + grad * sp[:, :, :, cols]

    dots = lax.fori_loop(
        0, tiles, norm_tile, jnp.zeros((frames, height, breadth, LANES), jnp.float32), unroll=2)
    mean = jnp.sum(dots, axis=-1, keepdims=True) * (1.0 / chans)

    def depth_tile(t, carry):
        cols = cols_of(t)
        grad = ag[:, cols].reshape(frames, height, breadth, LANES)
        sg = inv_rms * (grad - sp[:, :, :, cols] * mean)
        ag[:, cols] = sg.reshape(count, LANES)
        gs = [from_right(sg), sg, from_left(sg)]
        x = x_ref[0, :, :, :, cols].astype(jnp.float32)
        x0, x1 = x[:, 0], x[:, 1]
        for j in range(3):
            g0, g1 = gs[j][:, 0], gs[j][:, 1]
            for i, term in enumerate((x0 * g1, x0 * g0 + x1 * g1, x1 * g0)):
                dg[3 * i + j:3 * i + j + 1, cols] = jnp.sum(
                    jnp.sum(term, axis=0), axis=0, keepdims=True
                )
        return carry

    lax.fori_loop(0, tiles, depth_tile, 0, unroll=2)

    def grad_tile(t, carry):
        cols = cols_of(t)
        sg = ag[:, cols].reshape(frames, height, breadth, LANES)
        d = [d_full[k:k + 1, cols].reshape(1, 1, LANES) for k in range(9)]
        gs = [from_right(sg), sg, from_left(sg)]
        top = dy_ref[0, :, 0, :, cols].astype(jnp.float32)
        low = dy_ref[0, :, 1, :, cols].astype(jnp.float32)
        for j in range(3):
            g0, g1 = gs[j][:, 0], gs[j][:, 1]
            top = top + g0 * d[3 + j] + g1 * d[j]
            low = low + g0 * d[6 + j] + g1 * d[3 + j]
        gin_ref[0, :, 0, :, cols] = top.astype(jnp.bfloat16)
        gin_ref[0, :, 1, :, cols] = low.astype(jnp.bfloat16)
        return carry

    def dwin(p):
        return pl.ds(pl.multiple_of(LANES * (p + lax.div(p, 4)), LANES), 256)

    def p_copy(m, origin):
        return remote(
            dg_send.at[:, dwin(peers[m])], dg_recv.at[origin], sent.at[7], p_rs, shard=peers[m],
        )

    dg_send[...] = dg[...].astype(jnp.bfloat16)
    start([p_copy(m, me) for m in PEERS])
    dg_recv[me] = dg_send[:, dwin(me)]

    time_sum(0)
    lax.fori_loop(0, tiles, grad_tile, 0, unroll=2)
    for h in range(1, CHUNKS):
        time_sum(h)
    arrive(dg_recv.at[0:n - 1], p_rs)
    total = dg_recv[0].astype(jnp.float32)
    for p in range(1, n):
        total = total + dg_recv[p].astype(jnp.float32)
    dz_mine[...] = total
    start([
        remote(dz_mine, dz_recv.at[z], sent.at[8], q_rs, rep=zahead(r))
        for r in range(1, reps)
    ])
    dz_recv[z] = dz_mine[...]

    arrive(tem_all.at[0:(n - 1) * width, :], t_rs)

    def out_tile(t, carry):
        cols = cols_of(t)
        x = x_ref[0, :, :, :, cols].astype(jnp.float32)
        moved_on = tem_all[cols, :].astype(jnp.float32).T
        y = x + moved_on.reshape(frames, height, breadth, LANES)
        out_ref[0, :, :, :, cols] = y.astype(jnp.bfloat16)
        return carry

    lax.fori_loop(0, tiles, out_tile, 0, unroll=2)

    for h in range(CHUNKS):
        arrive(tg_out.at[h, 0:reps - 1], g_rs.at[h])
        grads = jnp.concatenate([tg_out[h, q].astype(jnp.float32) for q in range(reps)], axis=1)
        for k in range(3):
            tgrad_ref[k, piece * h:piece * (h + 1), :] = grads[:, k * width:(k + 1) * width]

    arrive(dz_recv.at[0:reps - 1], q_rs)
    whole = dz_recv[0]
    for r in range(1, reps):
        whole = whole + dz_recv[r]
    whole = pltpu.roll(whole * scale, lax.rem(256 - shift, 256), 1)
    dgrad_ref[...] = whole[0:9, 0:width]

    shard_bytes = cot_t.at[0:(n - 1) * width, :]
    amounts = (
        d_all.at[0:n - 1], shard_bytes, shard_bytes, shard_bytes, shard_bytes,
        tg_recv, tg_recv, dg_recv.at[0:n - 1], dz_recv.at[0:reps - 1],
    )
    for i, amount in enumerate(amounts):
        arrive(amount, sent.at[i])


def fused_device(latents, depth_taps, time_taps, cotangent):
    n, reps = lax.axis_size("shard"), lax.axis_size("rep")
    _, frames, height, breadth, chans = latents.shape
    count = frames * height * breadth
    width = chans // n
    bf, f32 = jnp.bfloat16, jnp.float32
    dma = pltpu.SemaphoreType.DMA
    piece, part = width // CHUNKS, 512 // reps
    vmem = pl.BlockSpec(memory_space=pltpu.VMEM)
    results = pl.pallas_call(
        functools.partial(fused_kernel, n, reps, 1.0 / (n * reps)),
        out_shape=(
            pltpu.VMEM(latents.shape, bf),
            pltpu.VMEM(latents.shape, bf),
            pltpu.VMEM((9, width), f32),
            pltpu.VMEM((3, width, width), f32),
        ),
        in_specs=[pl.BlockSpec(memory_space=pltpu.HBM)] * 4,
        out_specs=[vmem] * 4,
        scratch_shapes=[
            pltpu.VMEM(latents.shape, bf),
            pltpu.VMEM(depth_taps.shape, bf),
            pltpu.VMEM(time_taps.shape, bf),
            pltpu.VMEM(cotangent.shape, bf),
            dma((4,)),
            pltpu.VMEM((frames, height, breadth, chans), f32),
            pltpu.VMEM((frames, height, breadth, chans), f32),
            pltpu.VMEM((count, chans), f32),
            pltpu.VMEM((chans, count), bf),
            pltpu.VMEM((chans, count), bf),
            pltpu.VMEM((n, width, count), bf),
            pltpu.VMEM((n, width, count), bf),
            pltpu.VMEM((512, n * count), bf),
            pltpu.VMEM((3, width, width), bf),
            pltpu.VMEM((n, width, count), bf),
            pltpu.VMEM((chans, count), bf),
            pltpu.VMEM((n, width, count), bf),
            pltpu.VMEM((chans, count), bf),
            pltpu.VMEM((16, 256), bf),
            pltpu.VMEM((n, 16, 256), bf),
            pltpu.VMEM((16, chans), f32),
            pltpu.VMEM((CHUNKS, reps, piece, part), f32),
            pltpu.VMEM((CHUNKS, reps, piece, part), bf),
            pltpu.VMEM((CHUNKS, reps - 1, piece, part), bf),
            pltpu.VMEM((CHUNKS, reps, piece, part), bf),
            pltpu.VMEM((16, chans), f32),
            pltpu.VMEM((16, chans), bf),
            pltpu.VMEM((n, 16, 256), bf),
            pltpu.VMEM((16, 256), f32),
            pltpu.VMEM((reps, 16, 256), f32),
            dma((9,)), dma, dma((n // 2,)), dma((CHUNKS,)), dma, dma,
            dma((CHUNKS,)), dma((CHUNKS,)), dma, dma,
        ],
        compiler_params=pltpu.CompilerParams(
            collective_id=0, has_side_effects=True, vmem_limit_bytes=24 * 1024 * 1024
        ),
    )(*[pltpu.with_memory_space_constraint(a, pltpu.HBM)
        for a in (latents, depth_taps, time_taps, cotangent)])
    return store_out(results)


def store_kernel(*refs):
    sources, targets, sems = refs[:4], refs[4:8], refs[8]
    copies = [
        pltpu.make_async_copy(source, target, sems.at[i])
        for i, (source, target) in enumerate(zip(sources, targets))
    ]
    for copy in copies:
        copy.start()
    for copy in copies:
        copy.wait()


def store_out(results):
    return pl.pallas_call(
        store_kernel,
        out_shape=tuple(jax.ShapeDtypeStruct(r.shape, r.dtype) for r in results),
        in_specs=[pl.BlockSpec(memory_space=pltpu.VMEM)] * 4,
        out_specs=[pl.BlockSpec(memory_space=pltpu.HBM)] * 4,
        scratch_shapes=[pltpu.SemaphoreType.DMA((4,))],
        compiler_params=pltpu.CompilerParams(has_side_effects=True),
    )(*[pltpu.with_memory_space_constraint(r, pltpu.VMEM) for r in results])


def solution(mesh):
    placed = (
        P(("shard", "rep"), None, None, None, None),
        P(None, "shard"),
        P(None, None, "shard"),
        P(("shard", "rep"), None, None, None, None),
    )
    shards, reps = mesh.shape["shard"], mesh.shape["rep"]
    fused = shards == GROUPS and reps in (2, 4)
    return jax.shard_map(
        fused_device if fused else per_device,
        mesh=mesh,
        in_specs=placed,
        out_specs=(
            P(("shard", "rep"), None, None, None, None),
            P(("shard", "rep"), None, None, None, None),
            P(None, "shard"),
            P(None, None, "shard"),
        ),
        check_vma=False,
    )
```
